32 devices in a mesh: row: 4 (over y, x), col: 2 (over core), dp: 4 (over z).
Axes of the slice: x: 2, y: 2, z: 4, core: 2. Of those that a mesh axis runs over, the one named last changes fastest.
Arguments:
- out_grad: bfloat16 [4, 128, 4096], P('dp', 'col', 'row'), may hold values from -6 to 6
- saved_hidden: bfloat16 [4, 128, 14336], P('dp', 'row', 'col'), may hold values from -6 to 6
- down_weight: bfloat16 [14336, 4096], P(('col', 'dp'), 'row'), may hold values from -0.046875 to 0.046875
Outputs:
- hidden_grad: bfloat16 [4, 128, 14336], P('dp', 'row', 'col')
- weight_grad: bfloat16 [14336, 4096], P(('col', 'dp'), 'row')
The draws below stay inside these ranges and needn't reach their ends.
All inputs are finite; a program needn't handle non-finite values.
Results may differ from the reference program's by a relative error of at most 0.009.
Values may be sent and summed in bfloat16 or wider, within the bound.
A program may use at most 64 MiB of HBM per device.

```python
import jax
import jax.numpy as jnp
from jax import lax

D = 4096
FF = 14336
TOK_REP = 128
REPLICAS = 4
N_ROW = 4


def levels(key, shape, split, least, high):
    loudness = 1.0
    for dim, shards_of in split:
        heights = jax.random.uniform(jax.random.fold_in(jax.random.fold_in(key, 6), dim), (shards_of,), jnp.float32, least / len(split), high / len(split))
        loudness = loudness * jnp.repeat(jnp.exp(heights), shape[dim] // shards_of).reshape((-1,) + (1,) * (len(shape) - 1 - dim))
    return loudness


def bell_draw(rng, shape, deviation, reach, shards=(), kind=jnp.bfloat16):
    entries = deviation * jax.random.normal(rng, shape, jnp.float32)
    if shards:
        entries = entries * levels(rng, shape, shards, -0.22, 0.18)
    return jnp.clip(entries, -reach, reach).astype(kind)


def setup_inputs(seed: int = 0) -> dict:
    seeds = jax.random.split(jax.random.key(seed), 4)
    return {
        "out_grad": bell_draw(seeds[0], (REPLICAS, TOK_REP, D), 1.0, 6.0, ((0, 4), (1, 2), (2, 4))),
        "saved_hidden": bell_draw(seeds[1], (REPLICAS, TOK_REP, FF), 1.0, 6.0, ((0, 4), (1, 4), (2, 2))),
        "down_weight": bell_draw(seeds[2], (FF, D), FF ** -0.5, 0.046875, ((0, 8), (1, 4))),
    }


def reference(out_grad, saved_hidden, down_weight):
    width = D // N_ROW
    flat_grad = out_grad.reshape(REPLICAS * TOK_REP, D)
    flat_hidden = saved_hidden.reshape(REPLICAS * TOK_REP, FF)
    accum = jnp.zeros((REPLICAS * TOK_REP, FF), jnp.float32)
    for block in range(N_ROW):
        left = flat_grad[:, block * width:(block + 1) * width]
        right = down_weight[:, block * width:(block + 1) * width]
        partial_term = lax.dot_general(left, right, (((1,), (1,)), ((), ())), preferred_element_type=jnp.float32)
        rounded = lax.optimization_barrier(partial_term.astype(jnp.bfloat16))
        accum = accum + rounded.astype(jnp.float32)
    hidden_grad = accum.astype(jnp.bfloat16).reshape(REPLICAS, TOK_REP, FF)
    total = lax.dot_general(flat_hidden, flat_grad, (((0,), (0,)), ((), ())), preferred_element_type=jnp.float32)
    factor = jnp.float32(1.0) / jnp.sqrt(jnp.float32(REPLICAS * TOK_REP))
    weight_grad = (total * factor).astype(jnp.bfloat16)
    return (hidden_grad, weight_grad)
```

```python
import functools

import jax
import jax.numpy as jnp
import numpy as np
from jax import lax
from jax.experimental import pallas as pl
from jax.experimental.pallas import tpu as pltpu
from jax.sharding import PartitionSpec as P

MESH = pl.DeviceIdType.MESH


def by_collectives(out_grad, saved_hidden, down_weight):
    grad_local = out_grad[0]
    hidden_local = saved_hidden[0]
    units = down_weight.shape[0]
    width = down_weight.shape[1]
    grad_replica = lax.all_gather(grad_local, "col", axis=0, tiled=True)
    grad_all = lax.all_gather(grad_replica[:, None, :], "dp", axis=1, tiled=True)
    tok_count = grad_all.shape[0]
    replica_count = grad_all.shape[1]
    local_tokens = hidden_local.shape[0]
    hidden_units = lax.all_to_all(
        hidden_local[:, None, :], "dp", split_axis=2, concat_axis=1, tiled=True
    )
    factor = jnp.float32(1.0) / jnp.sqrt(jnp.float32(tok_count * replica_count))
    flat_grad = grad_all.reshape(tok_count * replica_count, width)
    rows = flat_grad
    summed = lax.psum_scatter(
        lax.dot_general(
            rows, down_weight, (((1,), (1,)), ((), ())), preferred_element_type=jnp.float32
        ).astype(jnp.bfloat16),
        "row",
        scatter_dimension=0,
        tiled=True,
    )
    local_grad = summed.reshape(local_tokens, replica_count, units)
    returned = lax.all_to_all(local_grad, "dp", split_axis=1, concat_axis=2, tiled=True)
    hidden_grad = returned.reshape(1, local_tokens, -1)
    rows = grad_all
    left = lax.all_gather(hidden_units, "row", axis=0, tiled=True).reshape(-1, units)
    right = rows.reshape(-1, width)
    total = lax.dot_general(
        left, right, (((0,), (0,)), ((), ())), preferred_element_type=jnp.float32
    )
    weight_grad = (total * factor).astype(jnp.bfloat16)
    return (hidden_grad, weight_grad)


def kernel(
    n_dp, n_row, factor,
    g, h, w, hg, wg,
    gfull, hfull, wv, part, rs, hsum, acc, wbuf,
    loc_sem, zg_s, zg_r, zh_s, zh_r, cg_s, cg_r, ag_s, ag_r, rs_s, rs_r, hz_s, hz_r, wo_sem,
):
    row = lax.axis_index("row")
    col = lax.axis_index("col")
    dp = lax.axis_index("dp")
    units, width = w.shape
    toks = h.shape[0]
    half = toks // 2
    tile = 256 if units % 256 == 0 else 128
    tiles = units // tile

    def dev(r=None, c=None, z=None):
        return {"row": row if r is None else r, "col": col if c is None else c,
                "dp": dp if z is None else z}

    def send(src, dst, ssem, rsem, to):
        cp = pltpu.make_async_remote_copy(
            src_ref=src, dst_ref=dst, send_sem=ssem, recv_sem=rsem,
            device_id=to, device_id_type=MESH)
        cp.start()
        return cp

    barrier = pltpu.get_barrier_semaphore()
    peers = [dev(c=1 - col)]
    peers += [dev(z=dp ^ k) for k in range(1, n_dp)]
    peers += [dev(r=row ^ j) for j in range(1, n_row)]
    for p in peers:
        pl.semaphore_signal(barrier, inc=1, device_id=p, device_id_type=MESH)

    def columns(z):
        return pl.ds(pl.multiple_of(z * units, 128), units)

    load_w = pltpu.make_async_copy(w, wv, loc_sem.at[0])
    load_g = pltpu.make_async_copy(g, gfull.at[0, col], loc_sem.at[1])
    load_h = pltpu.make_async_copy(h.at[:, columns(dp)], hfull.at[0, row], loc_sem.at[2])
    load_g.start()
    load_w.start()
    load_h.start()
    pl.semaphore_wait(barrier, len(peers))

    zg, zh, cg, agx, agy, fwx, fwy, hz = {}, {}, {}, {}, {}, {}, {}, {}
    rsc = {}
    cg[0] = send(g, gfull.at[0, col], cg_s.at[0], cg_r.at[0], dev(c=1 - col))
    for k in range(1, n_dp):
        zg[k] = send(g, gfull.at[k, col], zg_s.at[k], zg_r.at[k], dev(z=dp ^ k))

    def gather_own(k):
        src = h.at[:, columns(dp)] if k == 0 else hfull.at[k, row]
        agx[k] = send(src, hfull.at[k, row], ag_s.at[k, 0], ag_r.at[k, 0], dev(r=row ^ 1))
        agy[k] = send(src, hfull.at[k, row], ag_s.at[k, 1], ag_r.at[k, 1], dev(r=row ^ 2))

    def forward(k):
        agx[k].wait_recv()
        a = hfull.at[k, row ^ 1, pl.ds(0, half)]
        fwy[k] = send(a, a, ag_s.at[k, 2], ag_r.at[k, 2], dev(r=row ^ 2))
        agy[k].wait_recv()
        b = hfull.at[k, row ^ 2, pl.ds(half, half)]
        fwx[k] = send(b, b, ag_s.at[k, 3], ag_r.at[k, 3], dev(r=row ^ 1))

    gather_own(0)
    for k in range(1, n_dp):
        zh[k] = send(h.at[:, columns(dp ^ k)], hfull.at[k, row], zh_s.at[k], zh_r.at[k],
                     dev(z=dp ^ k))

    def partner(k):
        zg[k].wait_recv()
        src = gfull.at[k, col]
        cg[k] = send(src, src, cg_s.at[k], cg_r.at[k], dev(c=1 - col))

    def hidden_partial(j):
        lhs = gfull[2 * j:2 * j + 2].reshape(-1, width)

        @pl.loop(0, tiles)
        def _(i):
            at = pl.ds(pl.multiple_of(i * tile, tile), tile)
            res = lax.dot_general(lhs, wv[at, :], (((1,), (1,)), ((), ())),
                                  preferred_element_type=jnp.float32)
            part[2 * j:2 * j + 2, :, :, at] = res.astype(jnp.bfloat16).reshape(
                2, n_row, toks, tile)

        for k in (2 * j, 2 * j + 1):
            for q in range(1, n_row):
                rsc[k, q] = send(part.at[k, row ^ q], rs.at[k, q - 1], rs_s.at[k, q],
                                 rs_r.at[k, q], dev(r=row ^ q))

    def finish_hidden(k):
        for q in range(1, n_row):
            rsc[k, q].wait_recv()
        s = part[k, row].astype(jnp.float32)
        for q in range(1, n_row):
            s = s + rs[k, q - 1].astype(jnp.float32)
        hsum[k] = s.astype(jnp.bfloat16)
        dst = hg.at[:, columns(dp)]
        if k == 0:
            hz[0] = pltpu.make_async_copy(hsum.at[0], dst, loc_sem.at[3])
            hz[0].start()
        else:
            hz[k] = send(hsum.at[k], dst, hz_s.at[k], hz_r.at[k], dev(z=dp ^ k))

    def weight_part(j, first, last):
        for k in (2 * j, 2 * j + 1):
            fwx[k].wait_recv()
            fwy[k].wait_recv()
        rhs = gfull[2 * j:2 * j + 2].reshape(-1, width)

        @pl.loop(0, tiles)
        def _(i):
            at = pl.ds(pl.multiple_of(i * tile, tile), tile)
            lhs = hfull[2 * j:2 * j + 2, :, :, at].reshape(-1, tile)
            res = lax.dot_general(lhs, rhs, (((0,), (0,)), ((), ())),
                                  preferred_element_type=jnp.float32)
            if not first:
                res = acc[at, :] + res
            if last:
                wbuf[at, :] = (res * factor).astype(jnp.bfloat16)
                pltpu.make_async_copy(wbuf.at[at], wg.at[at], wo_sem.at[i]).start()
            else:
                acc[at, :] = res

    pairs = n_dp // 2
    load_w.wait()
    load_g.wait()
    load_h.wait()
    partner(1)
    cg[0].wait_recv()
    cg[1].wait_recv()
    hidden_partial(0)
    forward(0)
    zh[1].wait_recv()
    gather_own(1)
    for j in range(1, pairs):
        for k in (2 * j, 2 * j + 1):
            partner(k)
        for k in (2 * j, 2 * j + 1):
            cg[k].wait_recv()
        hidden_partial(j)
        forward(2 * j - 1)
        for k in (2 * j, 2 * j + 1):
            zh[k].wait_recv()
            gather_own(k)
        finish_hidden(2 * j - 1)
        finish_hidden(2 * j - 2)
        weight_part(j - 1, j == 1, False)
        forward(2 * j)
    forward(n_dp - 1)
    finish_hidden(n_dp - 1)
    finish_hidden(n_dp - 2)
    weight_part(pairs - 1, pairs == 1, True)

    for k in range(1, n_dp):
        hz[k].wait()
        zg[k].wait_send()
        zh[k].wait_send()
    hz[0].wait()
    for k in range(n_dp):
        for cp in (cg[k], agx[k], agy[k], fwx[k], fwy[k]):
            cp.wait_send()
        for q in range(1, n_row):
            rsc[k, q].wait_send()

    @pl.loop(0, tiles)
    def _(i):
        at = pl.ds(pl.multiple_of(i * tile, tile), tile)
        pltpu.make_async_copy(wbuf.at[at], wg.at[at], wo_sem.at[i]).wait()


def by_kernel(n_dp, n_row, out_grad, saved_hidden, down_weight):
    g, h, w = out_grad[0], saved_hidden[0], down_weight
    units, width = w.shape
    gt, toks = g.shape[0], h.shape[0]
    bf = jnp.bfloat16
    factor = np.float32(1.0) / np.sqrt(np.float32(n_dp * n_row * toks))
    dma = pltpu.SemaphoreType.DMA
    hg, wg = pl.pallas_call(
        functools.partial(kernel, n_dp, n_row, factor),
        out_shape=(jax.ShapeDtypeStruct(h.shape, bf), jax.ShapeDtypeStruct(w.shape, bf)),
        in_specs=[pl.BlockSpec(memory_space=pl.ANY)] * 3,
        out_specs=[pl.BlockSpec(memory_space=pl.ANY)] * 2,
        scratch_shapes=[
            pltpu.VMEM((n_dp, 2, gt, width), bf),
            pltpu.VMEM((n_dp, n_row, toks, units), bf),
            pltpu.VMEM((units, width), bf),
            pltpu.VMEM((n_dp, n_row, toks, units), bf),
            pltpu.VMEM((n_dp, n_row - 1, toks, units), bf),
            pltpu.VMEM((n_dp, toks, units), bf),
            pltpu.VMEM((units, width), jnp.float32),
            pltpu.VMEM((units, width), bf),
            dma((4,)), dma((n_dp,)), dma((n_dp,)), dma((n_dp,)), dma((n_dp,)),
            dma((n_dp,)), dma((n_dp,)), dma((n_dp, 4)), dma((n_dp, 4)),
            dma((n_dp, n_row)), dma((n_dp, n_row)), dma((n_dp,)), dma((n_dp,)),
            dma((units // 128,)),
        ],
        compiler_params=pltpu.CompilerParams(
            collective_id=0, has_side_effects=True, vmem_limit_bytes=48 * 1024 * 1024),
    )(g, h, w)
    return hg[None], wg


def solution(mesh):
    n_row, n_col, n_dp = mesh.shape["row"], mesh.shape["col"], mesh.shape["dp"]

    def on_device(out_grad, saved_hidden, down_weight):
        units = down_weight.shape[0]
        toks = saved_hidden.shape[1]
        fits = (n_row == 4 and n_col == 2 and n_dp in (2, 4, 8) and units % 128 == 0
                and toks % 32 == 0 and out_grad.shape[1] % 16 == 0)
        if not fits:
            return by_collectives(out_grad, saved_hidden, down_weight)
        return by_kernel(n_dp, n_row, out_grad, saved_hidden, down_weight)

    in_specs = (P("dp", "col", "row"), P("dp", "row", "col"), P(("col", "dp"), "row"))
    out_specs = (P("dp", "row", "col"), P(("col", "dp"), "row"))
    return jax.shard_map(
        on_device, mesh=mesh, in_specs=in_specs, out_specs=out_specs, check_vma=False
    )
```

```python
import functools

import jax
import jax.numpy as jnp
import numpy as np
from jax import lax
from jax.experimental import pallas as pl
from jax.experimental.pallas import tpu as pltpu
from jax.sharding import PartitionSpec as P

MESH = pl.DeviceIdType.MESH


def by_collectives(out_grad, saved_hidden, down_weight):
    grad_local = out_grad[0]
    hidden_local = saved_hidden[0]
    units = down_weight.shape[0]
    width = down_weight.shape[1]
    grad_replica = lax.all_gather(grad_local, "col", axis=0, tiled=True)
    grad_all = lax.all_gather(grad_replica[:, None, :], "dp", axis=1, tiled=True)
    tok_count = grad_all.shape[0]
    replica_count = grad_all.shape[1]
    local_tokens = hidden_local.shape[0]
    hidden_units = lax.all_to_all(
        hidden_local[:, None, :], "dp", split_axis=2, concat_axis=1, tiled=True
    )
    factor = jnp.float32(1.0) / jnp.sqrt(jnp.float32(tok_count * replica_count))
    flat_grad = grad_all.reshape(tok_count * replica_count, width)
    rows = flat_grad
    summed = lax.psum_scatter(
        lax.dot_general(
            rows, down_weight, (((1,), (1,)), ((), ())), preferred_element_type=jnp.float32
        ).astype(jnp.bfloat16),
        "row",
        scatter_dimension=0,
        tiled=True,
    )
    local_grad = summed.reshape(local_tokens, replica_count, units)
    returned = lax.all_to_all(local_grad, "dp", split_axis=1, concat_axis=2, tiled=True)
    hidden_grad = returned.reshape(1, local_tokens, -1)
    rows = grad_all
    left = lax.all_gather(hidden_units, "row", axis=0, tiled=True).reshape(-1, units)
    right = rows.reshape(-1, width)
    total = lax.dot_general(
        left, right, (((0,), (0,)), ((), ())), preferred_element_type=jnp.float32
    )
    weight_grad = (total * factor).astype(jnp.bfloat16)
    return (hidden_grad, weight_grad)


def kernel(
    n_dp, n_row, factor,
    g, h, w, hg, wg,
    gfull, hfull, wv, part, rx, ry, mid_out, mid_in, hsum, acc, wbuf,
    loc_sem, zg_s, zg_r, zf_s, zh_s, zh_r, cg_s, cg_r, ag_s, ag_r, rs_s, rs_r, hz_s, hz_r, wo_sem,
):
    row = lax.axis_index("row")
    col = lax.axis_index("col")
    dp = lax.axis_index("dp")
    ry_i, rx_i = row // 2, row % 2
    inner = jnp.logical_or(dp == 1, dp == 2)
    outer = jnp.logical_not(inner)
    units, width = w.shape
    toks = h.shape[0]
    half = toks // 2
    tile = 256 if units % 256 == 0 else 128
    tiles = units // tile

    def dev(r=None, c=None, z=None):
        return {"row": row if r is None else r, "col": col if c is None else c,
                "dp": dp if z is None else z}

    xn, yn, pn = dev(r=row ^ 1), dev(r=row ^ 2), dev(c=1 - col)

    def remote(src, dst, ssem, rsem, to):
        return pltpu.make_async_remote_copy(
            src_ref=src, dst_ref=dst, send_sem=ssem, recv_sem=rsem,
            device_id=to, device_id_type=MESH)

    def send(*args):
        cp = remote(*args)
        cp.start()
        return cp

    def columns(z):
        return pl.ds(pl.multiple_of(z * units, 128), units)

    barrier = pltpu.get_barrier_semaphore()
    peers = [pn] + [dev(z=dp ^ k) for k in range(1, n_dp)] + [xn, yn]
    for p in peers:
        pl.semaphore_signal(barrier, inc=1, device_id=p, device_id_type=MESH)
    load_g = pltpu.make_async_copy(g, gfull.at[0, col], loc_sem.at[1])
    load_w = pltpu.make_async_copy(w, wv, loc_sem.at[0])
    load_h = pltpu.make_async_copy(h.at[:, columns(dp)], hfull.at[0, row], loc_sem.at[2])
    load_g.start()
    load_w.start()
    load_h.start()
    pl.semaphore_wait(barrier, len(peers))

    agx, agy, fwx, fwy, hz = {}, {}, {}, {}, {}
    r1 = {}

    def grad_to(k):
        return remote(g, gfull.at[k, col], zg_s.at[k], zg_r.at[k], dev(z=dp ^ k))

    def grad_on(k_here, k_there, step):
        return remote(gfull.at[k_here, col], gfull.at[k_there, col], zf_s.at[k_here],
                      zg_r.at[k_there], dev(z=dp ^ step))

    def grad_pair(k):
        src = gfull.at[k, col]
        return remote(src, src, cg_s.at[k], cg_r.at[k], pn)

    def hidden_to(k):
        return remote(h.at[:, columns(dp ^ k)], hfull.at[k, row], zh_s.at[k], zh_r.at[k],
                      dev(z=dp ^ k))

    grad_to(1).start()

    @pl.when(inner)
    def _():
        grad_to(3).start()

    cg0 = send(g, gfull.at[0, col], cg_s.at[0], cg_r.at[0], pn)

    def gather_own(k):
        src = h.at[:, columns(dp)] if k == 0 else hfull.at[k, row]
        agx[k] = send(src, hfull.at[k, row], ag_s.at[k, 0], ag_r.at[k, 0], xn)
        agy[k] = send(src, hfull.at[k, row], ag_s.at[k, 1], ag_r.at[k, 1], yn)

    def forward(k):
        agx[k].wait_recv()
        a = hfull.at[k, row ^ 1, pl.ds(0, half)]
        fwy[k] = send(a, a, ag_s.at[k, 2], ag_r.at[k, 2], yn)
        agy[k].wait_recv()
        b = hfull.at[k, row ^ 2, pl.ds(half, half)]
        fwx[k] = send(b, b, ag_s.at[k, 3], ag_r.at[k, 3], xn)

    gather_own(0)

    def hidden_partial(lo, hi):
        lhs = gfull[lo:hi].reshape(-1, width)

        @pl.loop(0, tiles)
        def _(i):
            at = pl.ds(pl.multiple_of(i * tile, tile), tile)
            res = lax.dot_general(lhs, wv[at, :], (((1,), (1,)), ((), ())),
                                  preferred_element_type=jnp.float32)
            part[lo:hi, :, :, :, :, at] = res.astype(jnp.bfloat16).reshape(
                hi - lo, 2, 2, 2, half, tile)

        for k in range(lo, hi):
            r1[k, 0] = send(part.at[k, :, rx_i ^ 1, 0], rx.at[k], rs_s.at[k, 0],
                            rs_r.at[k, 0], xn)
            r1[k, 1] = send(part.at[k, ry_i ^ 1, :, 1], ry.at[k], rs_s.at[k, 1],
                            rs_r.at[k, 1], yn)

    f32, bf16 = jnp.float32, jnp.bfloat16

    def red_first(k):
        return remote(mid_out.at[k, 0], mid_in.at[k, 0], rs_s.at[k, 2], rs_r.at[k, 2], yn)

    def red_second(k):
        return remote(mid_out.at[k, 1], mid_in.at[k, 1], rs_s.at[k, 3], rs_r.at[k, 3], xn)

    def reduce_on(k):
        r1[k, 0].wait_recv()
        mid_out[k, 0] = (part[k, ry_i ^ 1, rx_i, 0].astype(f32)
                         + rx[k, ry_i ^ 1].astype(f32)).astype(bf16)
        red_first(k).start()
        r1[k, 1].wait_recv()
        mid_out[k, 1] = (part[k, ry_i, rx_i ^ 1, 1].astype(f32)
                         + ry[k, rx_i ^ 1].astype(f32)).astype(bf16)
        red_second(k).start()

    def finish_hidden(k):
        red_first(k).wait_recv()
        hsum[k, 0:half] = (part[k, ry_i, rx_i, 0].astype(f32) + rx[k, ry_i].astype(f32)
                           + mid_in[k, 0].astype(f32)).astype(bf16)
        red_second(k).wait_recv()
        hsum[k, half:toks] = (part[k, ry_i, rx_i, 1].astype(f32) + ry[k, rx_i].astype(f32)
                              + mid_in[k, 1].astype(f32)).astype(bf16)
        dst = hg.at[:, columns(dp)]
        if k == 0:
            hz[0] = pltpu.make_async_copy(hsum.at[0], dst, loc_sem.at[3])
            hz[0].start()
        else:
            hz[k] = send(hsum.at[k], dst, hz_s.at[k], hz_r.at[k], dev(z=dp ^ k))

    def weight_part(lo, hi, first, last):
        for k in range(lo, hi):
            fwx[k].wait_recv()
            fwy[k].wait_recv()
        rhs = gfull[lo:hi].reshape(-1, width)

        @pl.loop(0, tiles)
        def _(i):
            at = pl.ds(pl.multiple_of(i * tile, tile), tile)
            lhs = hfull[lo:hi, :, :, at].reshape(-1, tile)
            res = lax.dot_general(lhs, rhs, (((0,), (0,)), ((), ())),
                                  preferred_element_type=f32)
            if not first:
                res = acc[at, :] + res
            if last:
                wbuf[at, :] = (res * factor).astype(bf16)
                pltpu.make_async_copy(wbuf.at[at], wg.at[at], wo_sem.at[i]).start()
            else:
                acc[at, :] = res

    load_g.wait()
    grad_to(1).wait_recv()
    grad_pair(1).start()

    @pl.when(inner)
    def _():
        grad_on(1, 2, 3).start()
        grad_to(3).wait_recv()
        grad_on(3, 2, 1).start()
        grad_pair(3).start()

    load_h.wait()
    forward(0)

    @pl.when(inner)
    def _():
        grad_to(2).wait_recv()
        grad_on(2, 3, 1).start()
        grad_pair(2).start()
        for k in (3, 2, 1):
            hidden_to(k).start()

    load_w.wait()
    cg0.wait_recv()
    grad_pair(1).wait_recv()
    hidden_partial(0, 2)

    @pl.when(outer)
    def _():
        grad_to(2).wait_recv()
        grad_pair(2).start()
        for k in (1, 2, 3):
            hidden_to(k).start()

    grad_pair(2).wait_recv()
    hidden_partial(2, 3)

    @pl.when(outer)
    def _():
        reduce_on(0)
        grad_to(3).wait_recv()
        grad_pair(3).start()
        reduce_on(1)

    grad_pair(3).wait_recv()
    hidden_partial(3, 4)
    hidden_to(1).wait_recv()
    gather_own(1)
    weight_part(0, 1, True, False)
    reduce_on(2)
    reduce_on(3)
    for k in (2, 3):
        hidden_to(k).wait_recv()
        gather_own(k)
    forward(1)
    finish_hidden(2)
    finish_hidden(3)

    @pl.when(inner)
    def _():
        reduce_on(1)
        reduce_on(0)

    forward(2)
    forward(3)
    weight_part(1, 2, False, False)
    finish_hidden(1)
    finish_hidden(0)
    weight_part(2, 4, False, True)

    @pl.when(inner)
    def _():
        grad_to(3).wait_send()
        grad_on(1, 2, 3).wait_send()
        grad_on(3, 2, 1).wait_send()
        grad_on(2, 3, 1).wait_send()

    grad_to(1).wait_send()
    cg0.wait_send()
    hz[0].wait()
    for k in range(n_dp):
        if k:
            hz[k].wait()
            hidden_to(k).wait_send()
            grad_pair(k).wait_send()
        for cp in (agx[k], agy[k], fwx[k], fwy[k], r1[k, 0], r1[k, 1], red_first(k), red_second(k)):
            cp.wait_send()

    @pl.loop(0, tiles)
    def _(i):
        at = pl.ds(pl.multiple_of(i * tile, tile), tile)
        pltpu.make_async_copy(wbuf.at[at], wg.at[at], wo_sem.at[i]).wait()


def by_kernel(n_dp, n_row, out_grad, saved_hidden, down_weight):
    g, h, w = out_grad[0], saved_hidden[0], down_weight
    units, width = w.shape
    gt, toks = g.shape[0], h.shape[0]
    bf = jnp.bfloat16
    factor = np.float32(1.0) / np.sqrt(np.float32(n_dp * n_row * toks))
    dma = pltpu.SemaphoreType.DMA
    hg, wg = pl.pallas_call(
        functools.partial(kernel, n_dp, n_row, factor),
        out_shape=(jax.ShapeDtypeStruct(h.shape, bf), jax.ShapeDtypeStruct(w.shape, bf)),
        in_specs=[pl.BlockSpec(memory_space=pl.ANY)] * 3,
        out_specs=[pl.BlockSpec(memory_space=pl.ANY)] * 2,
        scratch_shapes=[
            pltpu.VMEM((n_dp, 2, gt, width), bf),
            pltpu.VMEM((n_dp, n_row, toks, units), bf),
            pltpu.VMEM((units, width), bf),
            pltpu.VMEM((n_dp, 2, 2, 2, toks // 2, units), bf),
            pltpu.VMEM((n_dp, 2, toks // 2, units), bf),
            pltpu.VMEM((n_dp, 2, toks // 2, units), bf),
            pltpu.VMEM((n_dp, 2, toks // 2, units), bf),
            pltpu.VMEM((n_dp, 2, toks // 2, units), bf),
            pltpu.VMEM((n_dp, toks, units), bf),
            pltpu.VMEM((units, width), jnp.float32),
            pltpu.VMEM((units, width), bf),
            dma((4,)), dma((n_dp,)), dma((n_dp,)), dma((n_dp,)), dma((n_dp,)), dma((n_dp,)),
            dma((n_dp,)), dma((n_dp,)), dma((n_dp, 4)), dma((n_dp, 4)),
            dma((n_dp, 4)), dma((n_dp, 4)), dma((n_dp,)), dma((n_dp,)),
            dma((units // 128,)),
        ],
        compiler_params=pltpu.CompilerParams(
            collective_id=0, has_side_effects=True, vmem_limit_bytes=62 * 1024 * 1024),
    )(g, h, w)
    return hg[None], wg


def solution(mesh):
    n_row, n_col, n_dp = mesh.shape["row"], mesh.shape["col"], mesh.shape["dp"]

    def on_device(out_grad, saved_hidden, down_weight):
        units = down_weight.shape[0]
        toks = saved_hidden.shape[1]
        fits = (n_row == 4 and n_col == 2 and n_dp == 4 and units % 128 == 0
                and toks % 32 == 0 and out_grad.shape[1] % 16 == 0)
        if not fits:
            return by_collectives(out_grad, saved_hidden, down_weight)
        return by_kernel(n_dp, n_row, out_grad, saved_hidden, down_weight)

    in_specs = (P("dp", "col", "row"), P("dp", "row", "col"), P(("col", "dp"), "row"))
    out_specs = (P("dp", "row", "col"), P(("col", "dp"), "row"))
    return jax.shard_map(
        on_device, mesh=mesh, in_specs=in_specs, out_specs=out_specs, check_vma=False
    )
```

```python
import functools

import jax
import jax.numpy as jnp
import numpy as np
from jax import lax
from jax.experimental import pallas as pl
from jax.experimental.pallas import tpu as pltpu
from jax.sharding import PartitionSpec as P

MESH = pl.DeviceIdType.MESH


def by_collectives(out_grad, saved_hidden, down_weight):
    grad_local = out_grad[0]
    hidden_local = saved_hidden[0]
    units = down_weight.shape[0]
    width = down_weight.shape[1]
    grad_replica = lax.all_gather(grad_local, "col", axis=0, tiled=True)
    grad_all = lax.all_gather(grad_replica[:, None, :], "dp", axis=1, tiled=True)
    tok_count = grad_all.shape[0]
    replica_count = grad_all.shape[1]
    local_tokens = hidden_local.shape[0]
    hidden_units = lax.all_to_all(
        hidden_local[:, None, :], "dp", split_axis=2, concat_axis=1, tiled=True
    )
    factor = jnp.float32(1.0) / jnp.sqrt(jnp.float32(tok_count * replica_count))
    flat_grad = grad_all.reshape(tok_count * replica_count, width)
    rows = flat_grad
    summed = lax.psum_scatter(
        lax.dot_general(
            rows, down_weight, (((1,), (1,)), ((), ())), preferred_element_type=jnp.float32
        ).astype(jnp.bfloat16),
        "row",
        scatter_dimension=0,
        tiled=True,
    )
    local_grad = summed.reshape(local_tokens, replica_count, units)
    returned = lax.all_to_all(local_grad, "dp", split_axis=1, concat_axis=2, tiled=True)
    hidden_grad = returned.reshape(1, local_tokens, -1)
    rows = grad_all
    left = lax.all_gather(hidden_units, "row", axis=0, tiled=True).reshape(-1, units)
    right = rows.reshape(-1, width)
    total = lax.dot_general(
        left, right, (((0,), (0,)), ((), ())), preferred_element_type=jnp.float32
    )
    weight_grad = (total * factor).astype(jnp.bfloat16)
    return (hidden_grad, weight_grad)


def kernel(
    n_dp, n_row, factor,
    g, h, w, hg, wg,
    gfull, hfull, wv, part, rx, ry, mid_out, mid_in, hsum, acc,
    loc_sem, zg_s, zg_r, zf_s, zh_s, zh_r, cg_s, cg_r, ag_s, ag_r, rs_s, rs_r, hz_s, hz_r,
):
    row = lax.axis_index("row")
    col = lax.axis_index("col")
    dp = lax.axis_index("dp")
    ry_i, rx_i = row // 2, row % 2
    inner = jnp.logical_or(dp == 1, dp == 2)
    outer = jnp.logical_not(inner)
    units, width = w.shape
    toks = h.shape[0]
    half = toks // 2
    tile = 256 if units % 256 == 0 else 128
    tiles = units // tile

    def dev(r=None, c=None, z=None):
        return {"row": row if r is None else r, "col": col if c is None else c,
                "dp": dp if z is None else z}

    xn, yn, pn = dev(r=row ^ 1), dev(r=row ^ 2), dev(c=1 - col)

    def remote(src, dst, ssem, rsem, to):
        return pltpu.make_async_remote_copy(
            src_ref=src, dst_ref=dst, send_sem=ssem, recv_sem=rsem,
            device_id=to, device_id_type=MESH)

    def send(*args):
        cp = remote(*args)
        cp.start()
        return cp

    def columns(z):
        return pl.ds(pl.multiple_of(z * units, 128), units)

    barrier = pltpu.get_barrier_semaphore()
    peers = [pn] + [dev(z=dp ^ k) for k in range(1, n_dp)] + [xn, yn]
    for p in peers:
        pl.semaphore_signal(barrier, inc=1, device_id=p, device_id_type=MESH)
    load_g = pltpu.make_async_copy(g, gfull.at[0, col], loc_sem.at[1])
    load_w = pltpu.make_async_copy(w, wv, loc_sem.at[0])
    load_h = pltpu.make_async_copy(h.at[:, columns(dp)], hfull.at[0, row], loc_sem.at[2])
    load_g.start()
    load_w.start()
    load_h.start()
    pl.semaphore_wait(barrier, len(peers))

    agx, agy, fwx, fwy = {}, {}, {}, {}
    r1 = {}

    def grad_to(k):
        return remote(g, gfull.at[k, col], zg_s.at[k], zg_r.at[k], dev(z=dp ^ k))

    def grad_on(k_here, k_there, step):
        return remote(gfull.at[k_here, col], gfull.at[k_there, col], zf_s.at[k_here],
                      zg_r.at[k_there], dev(z=dp ^ step))

    def grad_pair(k):
        src = gfull.at[k, col]
        return remote(src, src, cg_s.at[k], cg_r.at[k], pn)

    def hidden_to(k):
        return remote(h.at[:, columns(dp ^ k)], hfull.at[k, row], zh_s.at[k], zh_r.at[k],
                      dev(z=dp ^ k))

    grad_to(1).start()

    @pl.when(inner)
    def _():
        grad_to(3).start()

    cg0 = send(g, gfull.at[0, col], cg_s.at[0], cg_r.at[0], pn)

    def gather_own(k):
        src = h.at[:, columns(dp)] if k == 0 else hfull.at[k, row]
        agx[k] = send(src, hfull.at[k, row], ag_s.at[k, 0], ag_r.at[k, 0], xn)
        agy[k] = send(src, hfull.at[k, row], ag_s.at[k, 1], ag_r.at[k, 1], yn)

    def forward(k):
        agx[k].wait_recv()
        a = hfull.at[k, row ^ 1, pl.ds(0, half)]
        fwy[k] = send(a, a, ag_s.at[k, 2], ag_r.at[k, 2], yn)
        agy[k].wait_recv()
        b = hfull.at[k, row ^ 2, pl.ds(half, half)]
        fwx[k] = send(b, b, ag_s.at[k, 3], ag_r.at[k, 3], xn)

    gather_own(0)

    def hidden_partial(lo, hi):
        lhs = gfull[lo:hi].reshape(-1, width)

        @pl.loop(0, tiles)
        def _(i):
            at = pl.ds(pl.multiple_of(i * tile, tile), tile)
            res = lax.dot_general(lhs, wv[at, :], (((1,), (1,)), ((), ())),
                                  preferred_element_type=jnp.float32)
            part[lo:hi, :, :, :, :, at] = res.astype(jnp.bfloat16).reshape(
                hi - lo, 2, 2, 2, half, tile)

        for k in range(lo, hi):
            r1[k, 0] = send(part.at[k, :, rx_i ^ 1, 0], rx.at[k], rs_s.at[k, 0],
                            rs_r.at[k, 0], xn)
            r1[k, 1] = send(part.at[k, ry_i ^ 1, :, 1], ry.at[k], rs_s.at[k, 1],
                            rs_r.at[k, 1], yn)

    f32, bf16 = jnp.float32, jnp.bfloat16

    def red_first(k):
        return remote(mid_out.at[k, 0], mid_in.at[k, 0], rs_s.at[k, 2], rs_r.at[k, 2], yn)

    def red_second(k):
        return remote(mid_out.at[k, 1], mid_in.at[k, 1], rs_s.at[k, 3], rs_r.at[k, 3], xn)

    def reduce_on(k):
        r1[k, 0].wait_recv()
        mid_out[k, 0] = (part[k, ry_i ^ 1, rx_i, 0].astype(f32)
                         + rx[k, ry_i ^ 1].astype(f32)).astype(bf16)
        red_first(k).start()
        r1[k, 1].wait_recv()
        mid_out[k, 1] = (part[k, ry_i, rx_i ^ 1, 1].astype(f32)
                         + ry[k, rx_i ^ 1].astype(f32)).astype(bf16)
        red_second(k).start()

    def back_to(k):
        dst = hg.at[:, columns(dp)]
        if k == 0:
            return pltpu.make_async_copy(hsum.at[0], dst, loc_sem.at[3])
        return remote(hsum.at[k], dst, hz_s.at[k], hz_r.at[k], dev(z=dp ^ k))

    def finish_hidden(k):
        red_first(k).wait_recv()
        hsum[k, 0:half] = (part[k, ry_i, rx_i, 0].astype(f32) + rx[k, ry_i].astype(f32)
                           + mid_in[k, 0].astype(f32)).astype(bf16)
        red_second(k).wait_recv()
        hsum[k, half:toks] = (part[k, ry_i, rx_i, 1].astype(f32) + ry[k, rx_i].astype(f32)
                              + mid_in[k, 1].astype(f32)).astype(bf16)
        back_to(k).start()

    def weight_part(lo, hi, first, last):
        for k in range(lo, hi):
            fwx[k].wait_recv()
            fwy[k].wait_recv()
        rhs = gfull[lo:hi].reshape(-1, width)

        @pl.loop(0, tiles)
        def _(i):
            at = pl.ds(pl.multiple_of(i * tile, tile), tile)
            lhs = hfull[lo:hi, :, :, at].reshape(-1, tile)
            res = lax.dot_general(lhs, rhs, (((0,), (0,)), ((), ())),
                                  preferred_element_type=f32)
            if not first:
                res = acc[at, :] + res
            if last:
                wg[at, :] = (res * factor).astype(bf16)
            else:
                acc[at, :] = res

    load_g.wait()
    grad_to(1).wait_recv()
    grad_pair(1).start()

    @pl.when(inner)
    def _():
        grad_on(1, 2, 3).start()
        grad_to(3).wait_recv()
        grad_on(3, 2, 1).start()
        grad_pair(3).start()

    load_h.wait()
    forward(0)

    @pl.when(inner)
    def _():
        grad_to(2).wait_recv()
        grad_on(2, 3, 1).start()
        grad_pair(2).start()
        for k in (3, 2, 1):
            hidden_to(k).start()

    load_w.wait()
    cg0.wait_recv()
    grad_pair(1).wait_recv()
    hidden_partial(0, 2)

    @pl.when(outer)
    def _():
        grad_to(2).wait_recv()
        grad_pair(2).start()
        for k in (1, 2, 3):
            hidden_to(k).start()

    grad_pair(2).wait_recv()
    hidden_partial(2, 3)

    @pl.when(outer)
    def _():
        reduce_on(0)
        grad_to(3).wait_recv()
        grad_pair(3).start()
        reduce_on(1)

    grad_pair(3).wait_recv()
    hidden_partial(3, 4)
    @pl.when(inner)
    def _():
        reduce_on(0)
        reduce_on(1)

    weight_part(0, 1, True, False)
    reduce_on(2)
    hidden_to(1).wait_recv()
    gather_own(1)
    reduce_on(3)
    for k in (2, 3):
        hidden_to(k).wait_recv()
        gather_own(k)
    finish_hidden(1)
    finish_hidden(2)
    forward(1)
    finish_hidden(3)
    finish_hidden(0)
    forward(2)
    forward(3)
    weight_part(1, 2, False, False)
    weight_part(2, 4, False, True)

    @pl.when(inner)
    def _():
        grad_to(3).wait_send()
        grad_on(1, 2, 3).wait_send()
        grad_on(3, 2, 1).wait_send()
        grad_on(2, 3, 1).wait_send()

    grad_to(1).wait_send()
    cg0.wait_send()
    back_to(0).wait()
    for k in range(n_dp):
        if k:
            back_to(k).wait()
            hidden_to(k).wait_send()
            grad_pair(k).wait_send()
        for cp in (agx[k], agy[k], fwx[k], fwy[k], r1[k, 0], r1[k, 1], red_first(k), red_second(k)):
            cp.wait_send()


def by_kernel(n_dp, n_row, out_grad, saved_hidden, down_weight):
    g, h, w = (pltpu.with_memory_space_constraint(a, pltpu.HBM) for a in (out_grad[0], saved_hidden[0], down_weight))
    units, width = w.shape
    gt, toks = g.shape[0], h.shape[0]
    bf = jnp.bfloat16
    factor = np.float32(1.0) / np.sqrt(np.float32(n_dp * n_row * toks))
    dma = pltpu.SemaphoreType.DMA
    hg, wg = pl.pallas_call(
        functools.partial(kernel, n_dp, n_row, factor),
        out_shape=(jax.ShapeDtypeStruct(h.shape, bf), jax.ShapeDtypeStruct(w.shape, bf)),
        in_specs=[pl.BlockSpec(memory_space=pltpu.HBM)] * 3,
        out_specs=[pl.BlockSpec(memory_space=pl.ANY), pl.BlockSpec(memory_space=pltpu.VMEM)],
        scratch_shapes=[
            pltpu.VMEM((n_dp, 2, gt, width), bf),
            pltpu.VMEM((n_dp, n_row, toks, units), bf),
            pltpu.VMEM((units, width), bf),
            pltpu.VMEM((n_dp, 2, 2, 2, toks // 2, units), bf),
            pltpu.VMEM((n_dp, 2, toks // 2, units), bf),
            pltpu.VMEM((n_dp, 2, toks // 2, units), bf),
            pltpu.VMEM((n_dp, 2, toks // 2, units), bf),
            pltpu.VMEM((n_dp, 2, toks // 2, units), bf),
            pltpu.VMEM((n_dp, toks, units), bf),
            pltpu.VMEM((units, width), jnp.float32),
            dma((4,)), dma((n_dp,)), dma((n_dp,)), dma((n_dp,)), dma((n_dp,)), dma((n_dp,)),
            dma((n_dp,)), dma((n_dp,)), dma((n_dp, 4)), dma((n_dp, 4)),
            dma((n_dp, 4)), dma((n_dp, 4)), dma((n_dp,)), dma((n_dp,)),
        ],
        compiler_params=pltpu.CompilerParams(
            collective_id=0, has_side_effects=True, vmem_limit_bytes=44 * 1024 * 1024),
    )(g, h, w)
    return hg[None], wg


def solution(mesh):
    n_row, n_col, n_dp = mesh.shape["row"], mesh.shape["col"], mesh.shape["dp"]

    def on_device(out_grad, saved_hidden, down_weight):
        units = down_weight.shape[0]
        toks = saved_hidden.shape[1]
        fits = (n_row == 4 and n_col == 2 and n_dp == 4 and units % 128 == 0
                and toks % 32 == 0 and out_grad.shape[1] % 16 == 0)
        if not fits:
            return by_collectives(out_grad, saved_hidden, down_weight)
        return by_kernel(n_dp, n_row, out_grad, saved_hidden, down_weight)

    in_specs = (P("dp", "col", "row"), P("dp", "row", "col"), P(("col", "dp"), "row"))
    out_specs = (P("dp", "row", "col"), P(("col", "dp"), "row"))
    return jax.shard_map(
        on_device, mesh=mesh, in_specs=in_specs, out_specs=out_specs, check_vma=False
    )
```

```python
import functools

import jax
import jax.numpy as jnp
import numpy as np
from jax import lax
from jax.experimental import pallas as pl
from jax.experimental.pallas import tpu as pltpu
from jax.sharding import PartitionSpec as P

MESH = pl.DeviceIdType.MESH


def by_collectives(out_grad, saved_hidden, down_weight):
    grad_local = out_grad[0]
    hidden_local = saved_hidden[0]
    units = down_weight.shape[0]
    width = down_weight.shape[1]
    grad_replica = lax.all_gather(grad_local, "col", axis=0, tiled=True)
    grad_all = lax.all_gather(grad_replica[:, None, :], "dp", axis=1, tiled=True)
    tok_count = grad_all.shape[0]
    replica_count = grad_all.shape[1]
    local_tokens = hidden_local.shape[0]
    hidden_units = lax.all_to_all(
        hidden_local[:, None, :], "dp", split_axis=2, concat_axis=1, tiled=True
    )
    factor = jnp.float32(1.0) / jnp.sqrt(jnp.float32(tok_count * replica_count))
    flat_grad = grad_all.reshape(tok_count * replica_count, width)
    rows = flat_grad
    summed = lax.psum_scatter(
        lax.dot_general(
            rows, down_weight, (((1,), (1,)), ((), ())), preferred_element_type=jnp.float32
        ).astype(jnp.bfloat16),
        "row",
        scatter_dimension=0,
        tiled=True,
    )
    local_grad = summed.reshape(local_tokens, replica_count, units)
    returned = lax.all_to_all(local_grad, "dp", split_axis=1, concat_axis=2, tiled=True)
    hidden_grad = returned.reshape(1, local_tokens, -1)
    rows = grad_all
    left = lax.all_gather(hidden_units, "row", axis=0, tiled=True).reshape(-1, units)
    right = rows.reshape(-1, width)
    total = lax.dot_general(
        left, right, (((0,), (0,)), ((), ())), preferred_element_type=jnp.float32
    )
    weight_grad = (total * factor).astype(jnp.bfloat16)
    return (hidden_grad, weight_grad)


def kernel(
    n_dp, n_row, factor,
    g, h, w, hg, wg,
    gfull, hfull, wv, part, rx, ry, mid_out, mid_in, hsum, acc,
    loc_sem, zg_s, zg_r, zf_s, zh_s, zh_r, cg_s, cg_r, ag_s, ag_r, rs_s, rs_r, hz_s, hz_r,
):
    row = lax.axis_index("row")
    col = lax.axis_index("col")
    dp = lax.axis_index("dp")
    ry_i, rx_i = row // 2, row % 2
    inner = jnp.logical_or(dp == 1, dp == 2)
    outer = jnp.logical_not(inner)
    units, width = w.shape
    toks = h.shape[0]
    half = toks // 2
    tile = 256 if units % 256 == 0 else 128
    tiles = units // tile

    def dev(r=None, c=None, z=None):
        return {"row": row if r is None else r, "col": col if c is None else c,
                "dp": dp if z is None else z}

    xn, yn, pn = dev(r=row ^ 1), dev(r=row ^ 2), dev(c=1 - col)

    def remote(src, dst, ssem, rsem, to):
        return pltpu.make_async_remote_copy(
            src_ref=src, dst_ref=dst, send_sem=ssem, recv_sem=rsem,
            device_id=to, device_id_type=MESH)

    def send(*args):
        cp = remote(*args)
        cp.start()
        return cp

    def columns(z):
        return pl.ds(pl.multiple_of(z * units, 128), units)

    barrier = pltpu.get_barrier_semaphore()
    peers = [pn] + [dev(z=dp ^ k) for k in range(1, n_dp)] + [xn, yn]
    for p in peers:
        pl.semaphore_signal(barrier, inc=1, device_id=p, device_id_type=MESH)
    load_g = pltpu.make_async_copy(g, gfull.at[0, col], loc_sem.at[1])
    load_w = pltpu.make_async_copy(w, wv, loc_sem.at[0])
    load_h = pltpu.make_async_copy(h.at[:, columns(dp)], hfull.at[0, row], loc_sem.at[2])
    load_g.start()
    load_w.start()
    load_h.start()
    pl.semaphore_wait(barrier, len(peers))

    agx, agy, fwx, fwy = {}, {}, {}, {}
    r1 = {}

    def grad_to(k):
        return remote(g, gfull.at[k, col], zg_s.at[k], zg_r.at[k], dev(z=dp ^ k))

    def grad_on(k_here, k_there, step):
        return remote(gfull.at[k_here, col], gfull.at[k_there, col], zf_s.at[k_here],
                      zg_r.at[k_there], dev(z=dp ^ step))

    def grad_pair(k):
        src = gfull.at[k, col]
        return remote(src, src, cg_s.at[k], cg_r.at[k], pn)

    def hidden_to(k):
        return remote(h.at[:, columns(dp ^ k)], hfull.at[k, row], zh_s.at[k], zh_r.at[k],
                      dev(z=dp ^ k))

    grad_to(1).start()

    @pl.when(inner)
    def _():
        grad_to(3).start()

    cg0 = send(g, gfull.at[0, col], cg_s.at[0], cg_r.at[0], pn)

    def gather_own(k):
        src = h.at[:, columns(dp)] if k == 0 else hfull.at[k, row]
        agx[k] = send(src, hfull.at[k, row], ag_s.at[k, 0], ag_r.at[k, 0], xn)
        agy[k] = send(src, hfull.at[k, row], ag_s.at[k, 1], ag_r.at[k, 1], yn)

    def forward(k):
        agx[k].wait_recv()
        a = hfull.at[k, row ^ 1, pl.ds(0, half)]
        fwy[k] = send(a, a, ag_s.at[k, 2], ag_r.at[k, 2], yn)
        agy[k].wait_recv()
        b = hfull.at[k, row ^ 2, pl.ds(half, half)]
        fwx[k] = send(b, b, ag_s.at[k, 3], ag_r.at[k, 3], xn)

    gather_own(0)

    def hidden_partial(lo, hi):
        lhs = gfull[lo:hi].reshape(-1, width)

        @pl.loop(0, tiles)
        def _(i):
            at = pl.ds(pl.multiple_of(i * tile, tile), tile)
            res = lax.dot_general(lhs, wv[at, :], (((1,), (1,)), ((), ())),
                                  preferred_element_type=jnp.float32)
            part[lo:hi, :, :, :, :, at] = res.astype(jnp.bfloat16).reshape(
                hi - lo, 2, 2, 2, half, tile)

        for k in range(lo, hi):
            r1[k, 0] = send(part.at[k, :, rx_i ^ 1, 0], rx.at[k], rs_s.at[k, 0],
                            rs_r.at[k, 0], xn)
            r1[k, 1] = send(part.at[k, ry_i ^ 1, :, 1], ry.at[k], rs_s.at[k, 1],
                            rs_r.at[k, 1], yn)

    f32, bf16 = jnp.float32, jnp.bfloat16

    def red_first(k):
        return remote(mid_out.at[k, 0], mid_in.at[k, 0], rs_s.at[k, 2], rs_r.at[k, 2], yn)

    def red_second(k):
        return remote(mid_out.at[k, 1], mid_in.at[k, 1], rs_s.at[k, 3], rs_r.at[k, 3], xn)

    def reduce_on(k):
        r1[k, 0].wait_recv()
        mid_out[k, 0] = (part[k, ry_i ^ 1, rx_i, 0].astype(f32)
                         + rx[k, ry_i ^ 1].astype(f32)).astype(bf16)
        red_first(k).start()
        r1[k, 1].wait_recv()
        mid_out[k, 1] = (part[k, ry_i, rx_i ^ 1, 1].astype(f32)
                         + ry[k, rx_i ^ 1].astype(f32)).astype(bf16)
        red_second(k).start()

    def back_to(k):
        dst = hg.at[:, columns(dp)]
        if k == 0:
            return pltpu.make_async_copy(hsum.at[0], dst, loc_sem.at[3])
        return remote(hsum.at[k], dst, hz_s.at[k], hz_r.at[k], dev(z=dp ^ k))

    def finish_hidden(k):
        red_first(k).wait_recv()
        hsum[k, 0:half] = (part[k, ry_i, rx_i, 0].astype(f32) + rx[k, ry_i].astype(f32)
                           + mid_in[k, 0].astype(f32)).astype(bf16)
        red_second(k).wait_recv()
        hsum[k, half:toks] = (part[k, ry_i, rx_i, 1].astype(f32) + ry[k, rx_i].astype(f32)
                              + mid_in[k, 1].astype(f32)).astype(bf16)
        back_to(k).start()

    def weight_part(lo, hi, first, last):
        for k in range(lo, hi):
            fwx[k].wait_recv()
            fwy[k].wait_recv()
        rhs = gfull[lo:hi].reshape(-1, width)

        @pl.loop(0, tiles)
        def _(i):
            at = pl.ds(pl.multiple_of(i * tile, tile), tile)
            lhs = hfull[lo:hi, :, :, at].reshape(-1, tile)
            res = lax.dot_general(lhs, rhs, (((0,), (0,)), ((), ())),
                                  preferred_element_type=f32)
            if not first:
                res = acc[at, :] + res
            if last:
                wg[at, :] = (res * factor).astype(bf16)
            else:
                acc[at, :] = res

    load_g.wait()
    load_w.wait()
    cg0.wait_recv()
    hidden_partial(0, 1)
    grad_to(1).wait_recv()
    grad_pair(1).start()

    @pl.when(inner)
    def _():
        grad_on(1, 2, 3).start()
        grad_to(3).wait_recv()
        grad_on(3, 2, 1).start()
        grad_pair(3).start()

    load_h.wait()
    forward(0)

    @pl.when(inner)
    def _():
        grad_to(2).wait_recv()
        grad_on(2, 3, 1).start()
        grad_pair(2).start()
        for k in (3, 2, 1):
            hidden_to(k).start()

    grad_pair(1).wait_recv()
    hidden_partial(1, 2)

    @pl.when(outer)
    def _():
        grad_to(2).wait_recv()
        grad_pair(2).start()
        for k in (1, 2, 3):
            hidden_to(k).start()

    grad_pair(2).wait_recv()
    hidden_partial(2, 3)

    @pl.when(outer)
    def _():
        reduce_on(0)
        grad_to(3).wait_recv()
        grad_pair(3).start()
        reduce_on(1)

    grad_pair(3).wait_recv()
    hidden_to(1).wait_recv()
    gather_own(1)
    hidden_partial(3, 4)
    @pl.when(inner)
    def _():
        reduce_on(0)
        reduce_on(1)

    weight_part(0, 1, True, False)
    reduce_on(2)
    reduce_on(3)
    for k in (2, 3):
        hidden_to(k).wait_recv()
        gather_own(k)
    finish_hidden(1)
    finish_hidden(2)
    forward(1)
    finish_hidden(3)
    finish_hidden(0)
    forward(2)
    forward(3)
    weight_part(1, 2, False, False)
    weight_part(2, 4, False, True)

    @pl.when(inner)
    def _():
        grad_to(3).wait_send()
        grad_on(1, 2, 3).wait_send()
        grad_on(3, 2, 1).wait_send()
        grad_on(2, 3, 1).wait_send()

    grad_to(1).wait_send()
    cg0.wait_send()
    back_to(0).wait()
    for k in range(n_dp):
        if k:
            back_to(k).wait()
            hidden_to(k).wait_send()
            grad_pair(k).wait_send()
        for cp in (agx[k], agy[k], fwx[k], fwy[k], r1[k, 0], r1[k, 1], red_first(k), red_second(k)):
            cp.wait_send()


def by_kernel(n_dp, n_row, out_grad, saved_hidden, down_weight):
    g, h, w = (pltpu.with_memory_space_constraint(a, pltpu.HBM) for a in (out_grad[0], saved_hidden[0], down_weight))
    units, width = w.shape
    gt, toks = g.shape[0], h.shape[0]
    bf = jnp.bfloat16
    factor = np.float32(1.0) / np.sqrt(np.float32(n_dp * n_row * toks))
    dma = pltpu.SemaphoreType.DMA
    hg, wg = pl.pallas_call(
        functools.partial(kernel, n_dp, n_row, factor),
        out_shape=(jax.ShapeDtypeStruct(h.shape, bf), jax.ShapeDtypeStruct(w.shape, bf)),
        in_specs=[pl.BlockSpec(memory_space=pltpu.HBM)] * 3,
        out_specs=[pl.BlockSpec(memory_space=pl.ANY), pl.BlockSpec(memory_space=pltpu.VMEM)],
        scratch_shapes=[
            pltpu.VMEM((n_dp, 2, gt, width), bf),
            pltpu.VMEM((n_dp, n_row, toks, units), bf),
            pltpu.VMEM((units, width), bf),
            pltpu.VMEM((n_dp, 2, 2, 2, toks // 2, units), bf),
            pltpu.VMEM((n_dp, 2, toks // 2, units), bf),
            pltpu.VMEM((n_dp, 2, toks // 2, units), bf),
            pltpu.VMEM((n_dp, 2, toks // 2, units), bf),
            pltpu.VMEM((n_dp, 2, toks // 2, units), bf),
            pltpu.VMEM((n_dp, toks, units), bf),
            pltpu.VMEM((units, width), jnp.float32),
            dma((4,)), dma((n_dp,)), dma((n_dp,)), dma((n_dp,)), dma((n_dp,)), dma((n_dp,)),
            dma((n_dp,)), dma((n_dp,)), dma((n_dp, 4)), dma((n_dp, 4)),
            dma((n_dp, 4)), dma((n_dp, 4)), dma((n_dp,)), dma((n_dp,)),
        ],
        compiler_params=pltpu.CompilerParams(
            collective_id=0, has_side_effects=True, vmem_limit_bytes=44 * 1024 * 1024),
    )(g, h, w)
    return hg[None], wg


def solution(mesh):
    n_row, n_col, n_dp = mesh.shape["row"], mesh.shape["col"], mesh.shape["dp"]

    def on_device(out_grad, saved_hidden, down_weight):
        units = down_weight.shape[0]
        toks = saved_hidden.shape[1]
        fits = (n_row == 4 and n_col == 2 and n_dp == 4 and units % 128 == 0
                and toks % 32 == 0 and out_grad.shape[1] % 16 == 0)
        if not fits:
            return by_collectives(out_grad, saved_hidden, down_weight)
        return by_kernel(n_dp, n_row, out_grad, saved_hidden, down_weight)

    in_specs = (P("dp", "col", "row"), P("dp", "row", "col"), P(("col", "dp"), "row"))
    out_specs = (P("dp", "row", "col"), P(("col", "dp"), "row"))
    return jax.shard_map(
        on_device, mesh=mesh, in_specs=in_specs, out_specs=out_specs, check_vma=False
    )
```
